32 devices in a mesh: rows: 8 (over z, y), vocab: 4 (over x, core).
Axes of the slice: x: 2, y: 2, z: 4, core: 2. Of those that a mesh axis runs over, the one named last changes fastest.
Arguments:
- hidden_policy: bfloat16 [512, 1536], P('rows', 'vocab'), may hold values from -45 to 45
- hidden_reference: bfloat16 [512, 1536], P('rows', 'vocab'), may hold values from -45 to 45
- gain_policy: bfloat16 [1536], replicated, may hold values from 0.5 to 1.5
- gain_reference: bfloat16 [1536], replicated, may hold values from 0.5 to 1.5
- head_policy: bfloat16 [1536, 16384], P(None, ('rows', 'vocab')), may hold values from -20 to 20
- head_reference: bfloat16 [1536, 16384], P(None, ('rows', 'vocab')), may hold values from -20 to 20
- targets: int32 [512], P('rows'), may hold values from 0 to 16383
- loss_mask: int32 [512], P('rows'), may hold values from 0 to 1, as said below
- doc_lengths: int32 [16], replicated, may hold values from 1 to 127, as said below
- doc_owner: int32 [16], replicated, may hold values from 0 to 7, as said below
- doc_score: float32 [16], replicated, may hold values from -3 to 6
Outputs:
- token_logprob: float32 [1024], P('rows')
- doc_advantage: float32 [16], P('rows')
The draws below stay inside these ranges and needn't reach their ends.
Inputs may be any that keep to these rules, and one draw needn't show every extreme that they name: `loss_mask`: each index of rows holds at most 32 ones among its 64 tokens, and some index holds exactly 32. `doc_lengths`: documents lie end to end in the pack in this order; their lengths add up to 512. `doc_owner`: every index of rows owns exactly 2 documents, whose lengths add up to at most 128; for some index they add up to exactly 128.
All inputs are finite; a program needn't handle non-finite values.
Results may differ from the reference program's by a relative error of at most 0.0025.
Values may be sent and summed in bfloat16 or wider, within the bound.
A program may use at most 128 MiB of HBM per device.

```python
import math
import jax
import jax.numpy as jnp
from jax import lax

D = 1536
VOC_DEV = 512
TOK_DEV = 64
DOC_DEV = 2
TOKENS = 512
VOCAB = 16384
RESP_DEV = 32
CAP = 128
DOCS = 16
N_ROWS = 8


anchor_count = 4


anchor_strengths = (1.0, 1.7, 2.4, 3.0)


anchor_logit = 110.0


anchor_gap = 1.9


def doc_layout(key):
    stream = jax.random.fold_in(key, 11)
    key_one, key_two, key_three, key_four = jax.random.split(stream, 4)
    pairing = jax.random.permutation(key_one, N_ROWS)
    pair_count = N_ROWS // 2
    swing = jax.random.randint(key_two, (pair_count,), 0, TOK_DEV - DOC_DEV + 1)
    swing_one = swing[1] % (TOK_DEV - 2 * DOC_DEV + 1)
    larger = (TOK_DEV + swing).at[0].set(2 * TOK_DEV).at[1].set(TOK_DEV + swing_one)
    smaller = (TOK_DEV - swing).at[0].set(DOC_DEV).at[1].set(TOK_DEV - DOC_DEV - swing_one)
    totals = jnp.zeros((N_ROWS,), jnp.int32).at[pairing[0::2]].set(larger.astype(jnp.int32)).at[pairing[1::2]].set(smaller.astype(jnp.int32))
    weights = jax.random.randint(key_three, (N_ROWS, DOC_DEV), 1, 64)
    single_row = (jnp.arange(DOC_DEV, dtype=jnp.int32) == 0).astype(weights.dtype)
    weights = weights.at[pairing[0]].set(single_row)
    running = jnp.cumsum(weights, axis=1)
    cut_points = (totals[:, None] - DOC_DEV) * running // running[:, -1:]
    previous = jnp.concatenate([jnp.zeros((N_ROWS, 1), jnp.int32), cut_points[:, :-1].astype(jnp.int32)], axis=1)
    doc_lens = (1 + cut_points - previous).reshape(-1).astype(jnp.int32)
    owners = jnp.repeat(jnp.arange(N_ROWS, dtype=jnp.int32), DOC_DEV)
    shuffle = jax.random.permutation(key_four, DOCS)
    return (doc_lens[shuffle], owners[shuffle])


def anchor_set(key):
    anchors = jnp.clip(jax.random.normal(jax.random.fold_in(key, 90), (anchor_count, D), jnp.float32), -3.0, 3.0)
    positions = jax.random.permutation(jax.random.fold_in(key, 91), TOKENS)[:anchor_count]
    columns = jax.random.permutation(jax.random.fold_in(key, 92), VOCAB)[:2 * anchor_count]
    return (anchors, positions, columns)


def hidden_common(key, which):
    stream = jax.random.fold_in(key, 40 + which)
    key_one, key_two, key_three = jax.random.split(stream, 3)
    row_scale = jnp.exp(jax.random.uniform(key_two, (TOKENS, 1), jnp.float32, math.log(0.3), math.log(3.0)))
    col_scale = jnp.exp(jax.random.uniform(key_three, (1, D), jnp.float32, math.log(0.3), math.log(3.0)))
    values = jnp.clip(jax.random.normal(key_one, (TOKENS, D), jnp.float32), -4.0, 4.0) * row_scale * col_scale
    anchors, positions, columns = anchor_set(key)
    values = values.at[positions].set(anchors)
    return values.astype(jnp.bfloat16)


def head_common(key, which):
    stream = jax.random.fold_in(key, 60 + which)
    spread = 3.0 / math.sqrt(D)
    values = jnp.clip(jax.random.normal(stream, (D, VOCAB), jnp.float32), -4.0, 4.0) * spread
    anchors, positions, columns = anchor_set(key)
    strengths = jnp.array(anchor_strengths, jnp.float32)
    strong = anchors.T * strengths[None, :] * (anchor_logit / D)
    nearby = anchors.T * (strengths[None, :] - anchor_gap / anchor_logit) * (anchor_logit / D)
    values = values.at[:, columns[:anchor_count]].set(strong + 0.1 * values[:, columns[:anchor_count]])
    values = values.at[:, columns[anchor_count:]].set(nearby + 0.1 * values[:, columns[anchor_count:]])
    return values.astype(jnp.bfloat16)


def draw_hidden_policy(key, part):
    return hidden_common(key, 1)


def draw_hidden_reference(key, part):
    return hidden_common(key, 2)


def draw_head_policy(key, part):
    return head_common(key, 1)


def draw_head_reference(key, part):
    return head_common(key, 2)


def draw_loss_mask(key, part):
    stream = jax.random.fold_in(key, 21)
    key_one, key_two, key_three = jax.random.split(stream, 3)
    counts = jax.random.randint(key_one, (N_ROWS,), RESP_DEV - RESP_DEV // 2, RESP_DEV + 1)
    forced = jax.random.randint(key_two, (), 0, N_ROWS)
    counts = counts.at[forced].set(RESP_DEV)
    shuffled = jax.vmap(lambda subkey: jax.random.permutation(subkey, TOK_DEV))(jax.random.split(key_three, N_ROWS))
    return (shuffled < counts[:, None]).astype(jnp.int32).reshape(-1)


def draw_doc_lengths(key, part):
    doc_lens, owners = doc_layout(key)
    return doc_lens


def draw_doc_owner(key, part):
    doc_lens, owners = doc_layout(key)
    return owners


def draw_doc_score(key, part):
    doc_lens, owners = doc_layout(key)
    growth = 1.0 + 2.0 * owners.astype(jnp.float32) / (N_ROWS - 1)
    stream = jax.random.fold_in(key, 30)
    uniform_part = jax.random.uniform(stream, (DOCS,), jnp.float32, 0.5, 1.5)
    return uniform_part * growth


def with_ends(drawn, own_key, smallest, high):
    index_at = [jax.random.randint(jax.random.fold_in(own_key, axis), (), 0, length) for axis, length in enumerate(drawn.shape)]
    longest = drawn.shape.index(max(drawn.shape))
    next_to = index_at[:longest] + [(index_at[longest] + 1) % drawn.shape[longest]] + index_at[longest + 1:]
    return drawn.at[tuple(index_at)].set(smallest).at[tuple(next_to)].set(high)


def setup_inputs(seed: int = 0) -> dict:
    key_of = jax.random.split(jax.random.key(seed), 12)
    hidden_policy = draw_hidden_policy(jax.random.fold_in(key_of[11], 71), 0)
    hidden_reference = draw_hidden_reference(jax.random.fold_in(key_of[11], 71), 0)
    gain_policy = jnp.clip(1.0 + 0.1 * jax.random.normal(key_of[2], (D,), jnp.float32), 0.5, 1.5).astype(jnp.bfloat16)
    gain_reference = jnp.clip(1.0 + 0.1 * jax.random.normal(key_of[3], (D,), jnp.float32), 0.5, 1.5).astype(jnp.bfloat16)
    head_policy = draw_head_policy(jax.random.fold_in(key_of[11], 71), 0)
    head_reference = draw_head_reference(jax.random.fold_in(key_of[11], 71), 0)
    targets = with_ends(jax.random.randint(key_of[6], (TOKENS,), 0, VOCAB), jax.random.fold_in(key_of[6], 1), 0, VOCAB - 1).astype(jnp.int32)
    loss_mask = draw_loss_mask(jax.random.fold_in(key_of[11], 71), 0)
    doc_lengths = draw_doc_lengths(jax.random.fold_in(key_of[11], 71), 0)
    doc_owner = draw_doc_owner(jax.random.fold_in(key_of[11], 71), 0)
    doc_score = draw_doc_score(jax.random.fold_in(key_of[11], 71), 0)
    return {"hidden_policy": hidden_policy, "hidden_reference": hidden_reference, "gain_policy": gain_policy, "gain_reference": gain_reference, "head_policy": head_policy, "head_reference": head_reference, "targets": targets, "loss_mask": loss_mask, "doc_lengths": doc_lengths, "doc_owner": doc_owner, "doc_score": doc_score}


epsilon = 1e-06
kl_weight = 0.1

def final_norm(hidden, gain_vector):
    values = hidden.astype(jnp.float32)
    inverse_rms = lax.rsqrt(lax.optimization_barrier(jnp.mean(values * values, axis=1, keepdims=True)) + epsilon)
    return (values * inverse_rms * gain_vector.astype(jnp.float32)[None, :]).astype(jnp.bfloat16)

def token_logprobs(normed, head, targets):
    block_width = VOC_DEV * 8
    row_count = normed.shape[0]

    def advance(running, block_index):
        highest, exp_total = running
        head_block = lax.dynamic_slice_in_dim(head, block_index * block_width, block_width, 1)
        logits = jnp.dot(normed, head_block, preferred_element_type=jnp.float32)
        new_highest = jnp.maximum(highest, lax.optimization_barrier(jnp.max(logits, axis=1)))
        exp_total = exp_total * jnp.exp(highest - new_highest) + lax.optimization_barrier(jnp.sum(jnp.exp(logits - new_highest[:, None]), axis=1))
        return ((new_highest, exp_total), None)
    initial = (jnp.full((row_count,), -jnp.inf, jnp.float32), jnp.zeros((row_count,), jnp.float32))
    blocks = jnp.arange(head.shape[1] // block_width, dtype=jnp.int32)
    (highest, exp_total), _ = lax.scan(advance, initial, blocks)
    picked = jnp.take(head, targets, axis=1).astype(jnp.float32)
    target_logit = lax.optimization_barrier(jnp.sum(normed.astype(jnp.float32) * picked.T, axis=1))
    return target_logit - (highest + jnp.log(exp_total))

def doc_tables(doc_lengths, doc_owner):
    starts = (jnp.cumsum(doc_lengths) - doc_lengths).astype(jnp.int32)
    doc_order = jnp.arange(doc_lengths.shape[0], dtype=jnp.int32)
    before = ((doc_owner[None, :] == doc_owner[:, None]) & (doc_order[None, :] < doc_order[:, None])).astype(jnp.int32)
    offset = lax.optimization_barrier(jnp.sum(before * doc_lengths[None, :], axis=1)).astype(jnp.int32)
    doc_rank = lax.optimization_barrier(jnp.sum(before, axis=1)).astype(jnp.int32)
    return (starts, offset, doc_rank)

def slot_table(owner_index, starts, offset, doc_rank, doc_lengths, doc_owner, slot_count):
    slot_index = jnp.arange(slot_count, dtype=jnp.int32)[:, None]
    inside = ((doc_owner[None, :] == owner_index) & (slot_index >= offset[None, :]) & (slot_index < offset[None, :] + doc_lengths[None, :])).astype(jnp.int32)
    slot_token = lax.optimization_barrier(jnp.sum(inside * (starts[None, :] + slot_index - offset[None, :]), axis=1)).astype(jnp.int32)
    slot_filled = lax.optimization_barrier(jnp.sum(inside, axis=1)).astype(jnp.int32)
    slot_doc = lax.optimization_barrier(jnp.sum(inside * doc_rank[None, :], axis=1)).astype(jnp.int32)
    return (slot_token, slot_filled, slot_doc)

def document_rewards(policy_lp, reference_lp, slot_mask, slot_doc, owner_index, doc_owner, doc_rank, doc_score, doc_slots):
    weights_mask = slot_mask.astype(jnp.float32)
    log_ratio = policy_lp - reference_lp
    kl_term = 0.5 * log_ratio * log_ratio
    doc_number = jnp.arange(doc_slots, dtype=jnp.int32)[:, None]
    doc_pick = (slot_doc[None, :] == doc_number).astype(jnp.float32)
    counts = lax.optimization_barrier(jnp.sum(doc_pick * weights_mask[None, :], axis=1))
    kl_sum = lax.optimization_barrier(jnp.sum(doc_pick * (weights_mask * kl_term)[None, :], axis=1))
    chosen = ((doc_owner[None, :] == owner_index) & (doc_rank[None, :] == doc_number)).astype(jnp.float32)
    doc_value = lax.optimization_barrier(jnp.sum(chosen * doc_score[None, :], axis=1))
    reward = doc_value - kl_weight * kl_sum / jnp.maximum(counts, 1.0)
    return (reward, counts)

def reference(hidden_policy, hidden_reference, gain_policy, gain_reference, head_policy, head_reference, targets, loss_mask, doc_lengths, doc_owner, doc_score):
    normed_policy = final_norm(hidden_policy, gain_policy)
    normed_reference = final_norm(hidden_reference, gain_reference)
    logprob_policy = token_logprobs(normed_policy, head_policy, targets)
    logprob_reference = token_logprobs(normed_reference, head_reference, targets)
    starts, offset, doc_rank = doc_tables(doc_lengths, doc_owner)

    def per_owner(owner_index):
        slot_token, slot_filled, slot_doc = slot_table(owner_index, starts, offset, doc_rank, doc_lengths, doc_owner, CAP)
        slot_mask = jnp.take(loss_mask, slot_token) * slot_filled
        policy_lp = jnp.take(logprob_policy, slot_token)
        reference_lp = jnp.take(logprob_reference, slot_token)
        token_logprob = jnp.where(slot_mask == 1, policy_lp, 0.0)
        reward, counts = document_rewards(policy_lp, reference_lp, slot_mask, slot_doc, owner_index, doc_owner, doc_rank, doc_score, DOC_DEV)
        return (token_logprob, reward, counts)
    token_logprob, reward, counts = jax.vmap(per_owner)(jnp.arange(N_ROWS, dtype=jnp.int32))
    baseline = jnp.sum(counts * reward) / jnp.sum(counts)
    return (token_logprob.reshape(-1), (reward - baseline).reshape(-1))
```

```python
import functools

import jax
import jax.numpy as jnp
from jax import lax
from jax.experimental import pallas as pl
from jax.experimental.pallas import tpu as pltpu
from jax.sharding import PartitionSpec as P

DOC_DEV = 2
CAP = 128
RESP_DEV = 32

epsilon = 1e-06
kl_weight = 0.1
MESH = pl.DeviceIdType.MESH
F32 = jnp.float32
BF16 = jnp.bfloat16
LANES = 128


def iota(shape, dim):
    return lax.broadcasted_iota(jnp.int32, shape, dim)


def row_to_col(row):
    n = row.shape[1]
    return jnp.sum(jnp.where(iota((n, n), 0) == iota((n, n), 1), row, 0.0), axis=1, keepdims=True)


def col_to_row(col):
    n = col.shape[0]
    return jnp.sum(jnp.where(iota((n, n), 0) == iota((n, n), 1), col, 0.0), axis=0, keepdims=True)


def kernel(
    rows,
    vocab,
    hidden_p,
    hidden_r,
    gain_p,
    gain_r,
    head_p,
    head_r,
    targets,
    mask,
    lengths,
    owners,
    scores,
    out_lp,
    out_adv,
    heads,
    gathered,
    meta,
    stats,
    head_sem,
    send_sem,
    recv_sem,
    core_send,
    core_recv,
    meta_send,
    meta_recv,
    stat_send,
    stat_recv,
):
    Y, C = 2, 2
    Z, X = rows // Y, vocab // C
    tok, feat = hidden_p.shape
    resp = gathered.shape[4]
    n_tok = rows * resp
    vcols = heads.shape[2]
    r, v = lax.axis_index("rows"), lax.axis_index("vocab")
    z, y = r // Y, r % Y
    x, c = v // C, v % C
    devices = rows * vocab
    me = r * vocab + v

    head_copies = [
        pltpu.make_async_copy(src, heads.at[i], head_sem.at[i])
        for i, src in enumerate((head_p, head_r))
    ]
    for copy in head_copies:
        copy.start()

    barrier = pltpu.get_barrier_semaphore()
    for step in range(1, devices):
        other = (me + step) % devices
        pl.semaphore_signal(
            barrier, inc=1, device_id=(other // vocab, other % vocab), device_id_type=MESH
        )

    tri = (iota((tok, tok), 0) <= iota((tok, tok), 1)).astype(F32)

    def pick_of(mask_row):
        running = jnp.dot(
            jnp.broadcast_to(mask_row, (8, tok)).astype(BF16),
            tri.astype(BF16),
            preferred_element_type=F32,
        )[0:1]
        slots = iota((resp, tok), 0).astype(F32)
        return ((running - 1.0) == slots) & (mask_row == 1.0)

    own_mask = mask[...].astype(F32)
    own_pick = pick_of(own_mask).astype(BF16)
    for m, hidden in enumerate((hidden_p, hidden_r)):
        gathered[m, v, y, z] = jnp.dot(
            own_pick, hidden[...], preferred_element_type=F32
        ).astype(BF16)
    own_meta = y * Z + z
    meta[own_meta, 0:1, 0:tok] = targets[...]
    meta[own_meta, 1:2, 0:tok] = mask[...]
    pl.semaphore_wait(barrier, devices - 1)

    sends = []

    def block(m, ay, ax, d, core):
        return gathered.at[m, ((x + X - ax) % X) * C + core, (y + Y - ay) % Y, (z + Z - d) % Z]

    def remote(src, dst, s_sem, r_sem, dev):
        return pltpu.make_async_remote_copy(
            src_ref=src, dst_ref=dst, send_sem=s_sem, recv_sem=r_sem, device_id=dev, device_id_type=MESH
        )

    def send(m, held, moved, dev):
        src = block(m, *held, c)
        copy = remote(src, src, send_sem.at[(m, *moved)], recv_sem.at[(m, *moved)], dev)
        copy.start()
        sends.append(copy)

    def arrived(m, at):
        dst = block(m, *at, c)
        remote(dst, dst, send_sem.at[(m, *at)], recv_sem.at[(m, *at)], (r, v)).wait_recv()

    def to_core(m, at):
        src = block(m, *at, c)
        copy = remote(src, src, core_send.at[(m, *at)], core_recv.at[(m, *at)], (r, x * C + 1 - c))
        copy.start()
        sends.append(copy)

    for d in range(1, Z):
        for m in (0, 1):
            send(m, (0, 0, 0), (0, 0, d), (((z + d) % Z) * Y + y, v))
    for step in range(1, rows):
        other = (r + step) % rows
        copy = remote(
            meta.at[own_meta], meta.at[own_meta], meta_send.at[step], meta_recv.at[step], (other, v)
        )
        copy.start()
        sends.append(copy)

    def along_y(m, ax, d):
        send(m, (0, ax, d), (1, ax, d), (z * Y + 1 - y, v))

    def along_x(m, ay, d):
        for dx in range(1, X):
            send(m, (ay, 0, d), (ay, dx, d), (r, ((x + dx) % X) * C + c))

    for d in range(Z):
        for m in (0, 1):
            if d:
                arrived(m, (0, 0, d))
            if m == 0:
                along_y(m, 0, d)
            else:
                along_x(m, 0, d)
            to_core(m, (0, 0, d))
    for d in range(Z):
        along_x(0, 0, d)
        along_y(1, 0, d)
        arrived(0, (1, 0, d))
        along_x(0, 1, d)
        to_core(0, (1, 0, d))
        for dx in range(1, X):
            arrived(1, (0, dx, d))
            along_y(1, dx, d)
            to_core(1, (0, dx, d))
    for d in range(Z):
        for dx in range(1, X):
            for ay in range(Y):
                arrived(0, (ay, dx, d))
                to_core(0, (ay, dx, d))
        for dx in range(X):
            arrived(1, (1, dx, d))
            to_core(1, (1, dx, d))

    for step in range(1, rows):
        src = (r + rows - step) % rows
        slot = (src % Y) * Z + src // Y
        remote(
            meta.at[slot], meta.at[slot], meta_send.at[step], meta_recv.at[step], (r, v)
        ).wait_recv()
    target_cols, pos_cols, flag_cols = [], [], []
    for q in range(rows):
        pack = (q % Z) * Y + q // Z
        row_mask = meta[q, 1:2, 0:tok].astype(F32)
        pick = pick_of(row_mask)
        row_targets = meta[q, 0:1, 0:tok].astype(F32)
        where_at = (iota((1, tok), 1) + pack * tok).astype(F32)
        target_cols.append(jnp.sum(jnp.where(pick, row_targets, 0.0), axis=1, keepdims=True))
        pos_cols.append(jnp.sum(jnp.where(pick, where_at, 0.0), axis=1, keepdims=True))
        flag_cols.append(jnp.sum(jnp.where(pick, 1.0, 0.0), axis=1, keepdims=True))
    target_col = jnp.concatenate(target_cols, axis=0)
    pos_col = jnp.concatenate(pos_cols, axis=0)
    flag_col = jnp.concatenate(flag_cols, axis=0)
    base = (me * vcols).astype(F32)
    hit = iota((n_tok, vcols), 1).astype(F32) == (target_col - base)

    stat_cols = []
    for m, gain in enumerate((gain_p, gain_r)):
        for d in range(Z):
            for ay in range(Y):
                for ax in range(X):
                    dst = block(m, ay, ax, d, 1 - c)
                    remote(
                        dst, dst, core_send.at[m, ay, ax, d], core_recv.at[m, ay, ax, d], (r, v)
                    ).wait_recv()
        head_copies[m].wait()
        total = jnp.zeros((n_tok, 1), F32)
        for part in range(vocab):
            piece = gathered[m, part].reshape(n_tok, feat).astype(F32)
            total = total + jnp.sum(piece * piece, axis=1, keepdims=True)
        inverse_rms = lax.rsqrt(total / (feat * vocab) + epsilon)
        logits = jnp.zeros((n_tok, vcols), F32)
        for part in range(vocab):
            piece = gathered[m, part].reshape(n_tok, feat).astype(F32)
            weight = gain[0:1, part * feat : (part + 1) * feat].astype(F32)
            normed = (piece * inverse_rms * weight).astype(BF16)
            logits = logits + jnp.dot(
                normed, heads[m, part * feat : (part + 1) * feat, :], preferred_element_type=F32
            )
        highest = jnp.max(logits, axis=1, keepdims=True)
        lse = highest + jnp.log(jnp.sum(jnp.exp(logits - highest), axis=1, keepdims=True))
        stat_cols += [lse, jnp.sum(jnp.where(hit, logits, 0.0), axis=1, keepdims=True)]

    lane = iota((n_tok, LANES), 1)
    packed = jnp.zeros((n_tok, LANES), F32)
    for i, col in enumerate(stat_cols + [pos_col, flag_col]):
        packed = jnp.where(lane == i, col, packed)
    turned = jnp.transpose(packed)
    stats[me] = turned[0:4]
    pos, flag = turned[4:5], turned[5:6]

    docs = lengths.shape[1]
    length_row = lengths[...].astype(F32)
    owner_row = owners[...].astype(F32)
    length_col, owner_col = row_to_col(length_row), row_to_col(owner_row)
    score_col = row_to_col(scores[...])
    earlier = iota((docs, docs), 1) < iota((docs, docs), 0)
    starts = jnp.sum(jnp.where(earlier, length_row, 0.0), axis=1, keepdims=True)
    before = earlier & (owner_col == owner_row)
    offset = jnp.sum(jnp.where(before, length_row, 0.0), axis=1, keepdims=True)
    rank = jnp.sum(jnp.where(before, 1.0, 0.0), axis=1, keepdims=True)
    inside = (pos >= starts) & (pos < starts + length_col) & (flag == 1.0)
    counts = jnp.sum(jnp.where(inside, 1.0, 0.0), axis=1, keepdims=True)
    mine = owner_col == r.astype(F32)
    slot = jnp.sum(
        jnp.where(inside & mine, offset + pos - starts + 1.0, 0.0), axis=0, keepdims=True
    )
    lands = iota((CAP, n_tok), 0).astype(F32) == slot - 1.0

    for step in range(1, devices):
        other = (me + step) % devices
        copy = remote(
            stats.at[me],
            stats.at[me],
            stat_send.at[step],
            stat_recv.at[step],
            (other // vocab, other % vocab),
        )
        copy.start()
        sends.append(copy)
    for step in range(1, devices):
        src = (me + devices - step) % devices
        remote(
            stats.at[src], stats.at[src], stat_send.at[step], stat_recv.at[step], (r, v)
        ).wait_recv()

    every = stats[...]
    top = jnp.max(every, axis=0)
    spread = jnp.log(jnp.sum(jnp.exp(every - top[None]), axis=0)) + top
    summed = jnp.sum(every, axis=0)
    lp_p = summed[1:2] - spread[0:1]
    lp_r = summed[3:4] - spread[2:3]
    ratio = lp_p - lp_r
    kl = 0.5 * ratio * ratio
    kl_sum = jnp.sum(jnp.where(inside, kl, 0.0), axis=1, keepdims=True)
    reward = score_col - kl_weight * kl_sum / jnp.maximum(counts, 1.0)
    baseline = jnp.sum(counts * reward, axis=0, keepdims=True) / jnp.sum(
        counts, axis=0, keepdims=True
    )
    advantage = reward - baseline
    lane_doc = iota((docs, LANES), 1).astype(F32)
    out_adv[...] = jnp.sum(
        jnp.where(mine & (rank == lane_doc), advantage, 0.0), axis=0, keepdims=True
    )
    out_lp[...] = col_to_row(jnp.sum(jnp.where(lands, lp_p, 0.0), axis=1, keepdims=True))
    for copy in sends:
        copy.wait_send()


def per_device(
    rows,
    vocab,
    hidden_policy,
    hidden_reference,
    gain_policy,
    gain_reference,
    head_policy,
    head_reference,
    targets,
    loss_mask,
    doc_lengths,
    doc_owner,
    doc_score,
):
    row = lambda a: a.reshape(1, a.shape[0])
    feat = hidden_policy.shape[1]
    width, vcols = head_policy.shape
    z, x = rows // 2, vocab // 2
    n_tok = rows * RESP_DEV
    devices = rows * vocab
    vmem = pl.BlockSpec(memory_space=pltpu.VMEM)
    hbm = pl.BlockSpec(memory_space=pl.ANY)
    dma = pltpu.SemaphoreType.DMA
    lp, adv = pl.pallas_call(
        functools.partial(kernel, rows, vocab),
        out_shape=(
            jax.ShapeDtypeStruct((1, CAP), F32),
            jax.ShapeDtypeStruct((1, LANES), F32),
        ),
        in_specs=[vmem] * 4 + [hbm] * 2 + [vmem] * 5,
        out_specs=(vmem, vmem),
        scratch_shapes=[
            pltpu.VMEM((2, width, vcols), BF16),
            pltpu.VMEM((2, vocab, 2, z, RESP_DEV, feat), BF16),
            pltpu.VMEM((rows, 2, LANES), jnp.int32),
            pltpu.VMEM((devices, 4, n_tok), F32),
            dma((2,)),
            dma((2, 2, x, z)),
            dma((2, 2, x, z)),
            dma((2, 2, x, z)),
            dma((2, 2, x, z)),
            dma((rows,)),
            dma((rows,)),
            dma((devices,)),
            dma((devices,)),
        ],
        compiler_params=pltpu.CompilerParams(
            collective_id=0, has_side_effects=True, vmem_limit_bytes=60 * 1024 * 1024
        ),
    )(
        hidden_policy,
        hidden_reference,
        row(gain_policy),
        row(gain_reference),
        head_policy,
        head_reference,
        row(targets),
        row(loss_mask),
        row(doc_lengths),
        row(doc_owner),
        row(doc_score),
    )
    return lp.reshape(CAP), adv[0, :DOC_DEV]


def solution(mesh):
    return jax.shard_map(
        functools.partial(per_device, mesh.shape["rows"], mesh.shape["vocab"]),
        mesh=mesh,
        in_specs=(
            P("rows", "vocab"),
            P("rows", "vocab"),
            P(),
            P(),
            P(None, ("rows", "vocab")),
            P(None, ("rows", "vocab")),
            P("rows"),
            P("rows"),
            P(),
            P(),
            P(),
        ),
        out_specs=(P("rows"), P("rows")),
        check_vma=False,
    )
```

```python
import functools

import jax
import jax.numpy as jnp
from jax import lax
from jax.experimental import pallas as pl
from jax.experimental.pallas import tpu as pltpu
from jax.sharding import PartitionSpec as P

DOC_DEV = 2
CAP = 128
RESP_DEV = 32

epsilon = 1e-06
kl_weight = 0.1
MESH = pl.DeviceIdType.MESH
F32 = jnp.float32
BF16 = jnp.bfloat16
LANES = 128


def iota(shape, dim):
    return lax.broadcasted_iota(jnp.int32, shape, dim)


def row_to_col(row):
    n = row.shape[1]
    return jnp.sum(jnp.where(iota((n, n), 0) == iota((n, n), 1), row, 0.0), axis=1, keepdims=True)


def col_to_row(col):
    n = col.shape[0]
    return jnp.sum(jnp.where(iota((n, n), 0) == iota((n, n), 1), col, 0.0), axis=0, keepdims=True)


def kernel(
    rows,
    vocab,
    hidden_p,
    hidden_r,
    gain_p,
    gain_r,
    head_p,
    head_r,
    targets,
    mask,
    lengths,
    owners,
    scores,
    out_lp,
    out_adv,
    heads,
    gathered,
    meta,
    stats,
    head_sem,
    send_sem,
    recv_sem,
    core_send,
    core_recv,
    line_send,
    meta_send,
    meta_recv,
    stat_send,
    stat_recv,
):
    Y, C = 2, 2
    Z, X = rows // Y, vocab // C
    tok, feat = hidden_p.shape
    resp = gathered.shape[4]
    n_tok = rows * resp
    vcols = heads.shape[2]
    r, v = lax.axis_index("rows"), lax.axis_index("vocab")
    z, y = r // Y, r % Y
    x, c = v // C, v % C
    devices = rows * vocab
    me = r * vocab + v

    head_copies = [
        pltpu.make_async_copy(src, heads.at[i], head_sem.at[i])
        for i, src in enumerate((head_p, head_r))
    ]
    for copy in head_copies:
        copy.start()

    barrier = pltpu.get_barrier_semaphore()

    def greet(dev):
        pl.semaphore_signal(barrier, inc=1, device_id=dev, device_id_type=MESH)

    greet((r, x * C + 1 - c))
    greet((z * Y + 1 - y, v))
    for dx in range(1, X):
        greet((r, ((x + dx) % X) * C + c))
    for step in range(1, Z):
        greet((((z + step) % Z) * Y + y, v))

    tri = (iota((tok, tok), 0) <= iota((tok, tok), 1)).astype(F32)

    def pick_of(mask_row):
        running = jnp.dot(
            jnp.broadcast_to(mask_row, (8, tok)).astype(BF16),
            tri.astype(BF16),
            preferred_element_type=F32,
        )[0:1]
        slots = iota((resp, tok), 0).astype(F32)
        return ((running - 1.0) == slots) & (mask_row == 1.0)

    own_mask = mask[...].astype(F32)
    own_pick = pick_of(own_mask).astype(BF16)
    for m, hidden in enumerate((hidden_p, hidden_r)):
        gathered[m, v, y, z] = jnp.dot(
            own_pick, hidden[...], preferred_element_type=F32
        ).astype(BF16)
    own_meta = y * Z + z
    meta[own_meta, 0:1, 0:tok] = targets[...]
    meta[own_meta, 1:2, 0:tok] = mask[...]
    pl.semaphore_wait(barrier, X + Z)

    sends = []

    near = jnp.minimum(z, Z - 1 - z)
    order = [z]
    for t in range(1, Z):
        paired = z - (t + 1) // 2 if t % 2 else z + t // 2
        beyond = jnp.where(z > Z - 1 - z, z - (t - near), z + (t - near))
        order.append(jnp.where(t <= 2 * near, paired, beyond))

    def block(m, ay, ax, zz, core):
        return gathered.at[m, ((x + X - ax) % X) * C + core, (y + Y - ay) % Y, zz]

    def remote(src, dst, s_sem, r_sem, dev):
        return pltpu.make_async_remote_copy(
            src_ref=src, dst_ref=dst, send_sem=s_sem, recv_sem=r_sem, device_id=dev, device_id_type=MESH
        )

    def start(ref, s_sem, r_sem, dev):
        copy = remote(ref, ref, s_sem, r_sem, dev)
        copy.start()
        sends.append(copy)

    def send(m, held, moved, zz, dev):
        start(block(m, *held, zz, c), send_sem.at[(m, *moved, zz)], recv_sem.at[(m, *moved, zz)], dev)

    def landed(ref, s_sem, r_sem):
        remote(ref, ref, s_sem, r_sem, (r, v)).wait_recv()

    def arrived(m, ay, ax, zz):
        landed(block(m, ay, ax, zz, c), send_sem.at[m, ay, ax, zz], recv_sem.at[m, ay, ax, zz])

    def to_core(m, ay, ax, zz):
        start(
            block(m, ay, ax, zz, c),
            core_send.at[m, ay, ax, zz],
            core_recv.at[m, ay, ax, zz],
            (r, x * C + 1 - c),
        )

    def along_y(m, ax, zz):
        send(m, (0, ax), (1, ax), zz, (z * Y + 1 - y, v))

    def along_x(m, ay, zz):
        for dx in range(1, X):
            send(m, (ay, 0), (ay, dx), zz, (r, ((x + dx) % X) * C + c))

    def meta_at(ay, zz):
        return meta.at[((y + Y - ay) % Y) * Z + zz]

    def pass_on(t, zz, part):
        if t:
            return
        ref = meta_at(0, zz) if part == 2 else block(part, 0, 0, zz, c)
        r_sem = meta_recv.at[0, zz] if part == 2 else recv_sem.at[part, 0, 0, zz]
        for step in range(1, Z):
            start(ref, line_send.at[part * Z + step], r_sem, (((z + step) % Z) * Y + y, v))

    def second(zz):
        arrived(0, 1, 0, zz)
        along_x(0, 1, zz)
        to_core(0, 1, 0, zz)
        for dx in range(1, X):
            arrived(1, 0, dx, zz)
            along_y(1, dx, zz)
            to_core(1, 0, dx, zz)

    for t, zz in enumerate(order):
        for m in (0, 1):
            if t:
                arrived(m, 0, 0, zz)
            pass_on(t, zz, m)
            if m == 0:
                along_y(0, 0, zz)
            else:
                along_x(1, 0, zz)
                along_x(0, 0, zz)
                along_y(1, 0, zz)
        if t:
            landed(meta_at(0, zz), meta_send.at[0, zz], meta_recv.at[0, zz])
        pass_on(t, zz, 2)
        start(meta_at(0, zz), meta_send.at[1, zz], meta_recv.at[1, zz], (z * Y + 1 - y, v))
        to_core(0, 0, 0, zz)
        to_core(1, 0, 0, zz)
    for zz in order:
        second(zz)
    for zz in order:
        for dx in range(1, X):
            for ay in range(Y):
                arrived(0, ay, dx, zz)
                to_core(0, ay, dx, zz)
        for dx in range(X):
            arrived(1, 1, dx, zz)
            to_core(1, 1, dx, zz)

    for zz in order:
        landed(meta_at(1, zz), meta_send.at[1, zz], meta_recv.at[1, zz])
    target_cols, pos_cols, flag_cols = [], [], []
    for q in range(rows):
        pack = (q % Z) * Y + q // Z
        row_mask = meta[q, 1:2, 0:tok].astype(F32)
        pick = pick_of(row_mask)
        row_targets = meta[q, 0:1, 0:tok].astype(F32)
        where_at = (iota((1, tok), 1) + pack * tok).astype(F32)
        target_cols.append(jnp.sum(jnp.where(pick, row_targets, 0.0), axis=1, keepdims=True))
        pos_cols.append(jnp.sum(jnp.where(pick, where_at, 0.0), axis=1, keepdims=True))
        flag_cols.append(jnp.sum(jnp.where(pick, 1.0, 0.0), axis=1, keepdims=True))
    target_col = jnp.concatenate(target_cols, axis=0)
    pos_col = jnp.concatenate(pos_cols, axis=0)
    flag_col = jnp.concatenate(flag_cols, axis=0)
    base = (me * vcols).astype(F32)
    hit = iota((n_tok, vcols), 1).astype(F32) == (target_col - base)

    stat_cols = []
    for m, gain in enumerate((gain_p, gain_r)):
        for zz in order:
            for ay in range(Y):
                for ax in range(X):
                    landed(
                        block(m, ay, ax, zz, 1 - c),
                        core_send.at[m, ay, ax, zz],
                        core_recv.at[m, ay, ax, zz],
                    )
        head_copies[m].wait()
        total = jnp.zeros((n_tok, 1), F32)
        for part in range(vocab):
            piece = gathered[m, part].reshape(n_tok, feat).astype(F32)
            total = total + jnp.sum(piece * piece, axis=1, keepdims=True)
        inverse_rms = lax.rsqrt(total / (feat * vocab) + epsilon)
        logits = jnp.zeros((n_tok, vcols), F32)
        for part in range(vocab):
            piece = gathered[m, part].reshape(n_tok, feat).astype(F32)
            weight = gain[pl.ds(part * feat, feat)].astype(F32).reshape(1, feat)
            normed = (piece * inverse_rms * weight).astype(BF16)
            logits = logits + jnp.dot(
                normed, heads[m, part * feat : (part + 1) * feat, :], preferred_element_type=F32
            )
        highest = jnp.max(logits, axis=1, keepdims=True)
        lse = highest + jnp.log(jnp.sum(jnp.exp(logits - highest), axis=1, keepdims=True))
        stat_cols += [lse, jnp.sum(jnp.where(hit, logits, 0.0), axis=1, keepdims=True)]

    lane = iota((n_tok, LANES), 1)
    packed = jnp.zeros((n_tok, LANES), F32)
    for i, col in enumerate(stat_cols + [pos_col, flag_col]):
        packed = jnp.where(lane == i, col, packed)
    turned = jnp.transpose(packed)
    stats[me] = turned[0:4]
    pos, flag = turned[4:5], turned[5:6]

    docs = lengths.shape[1]
    length_row = lengths[...].astype(F32)
    owner_row = owners[...].astype(F32)
    length_col, owner_col = row_to_col(length_row), row_to_col(owner_row)
    score_col = row_to_col(scores[...])
    earlier = iota((docs, docs), 1) < iota((docs, docs), 0)
    starts = jnp.sum(jnp.where(earlier, length_row, 0.0), axis=1, keepdims=True)
    before = earlier & (owner_col == owner_row)
    offset = jnp.sum(jnp.where(before, length_row, 0.0), axis=1, keepdims=True)
    rank = jnp.sum(jnp.where(before, 1.0, 0.0), axis=1, keepdims=True)
    inside = (pos >= starts) & (pos < starts + length_col) & (flag == 1.0)
    counts = jnp.sum(jnp.where(inside, 1.0, 0.0), axis=1, keepdims=True)
    mine = owner_col == r.astype(F32)
    slot = jnp.sum(
        jnp.where(inside & mine, offset + pos - starts + 1.0, 0.0), axis=0, keepdims=True
    )
    lands = iota((CAP, n_tok), 0).astype(F32) == slot - 1.0

    for step in range(1, devices):
        other = (me + step) % devices
        copy = remote(
            stats.at[me],
            stats.at[me],
            stat_send.at[step],
            stat_recv.at[step],
            (other // vocab, other % vocab),
        )
        copy.start()
        sends.append(copy)
    for step in range(1, devices):
        src = (me + devices - step) % devices
        remote(
            stats.at[src], stats.at[src], stat_send.at[step], stat_recv.at[step], (r, v)
        ).wait_recv()

    every = stats[...]
    top = jnp.max(every, axis=0)
    spread = jnp.log(jnp.sum(jnp.exp(every - top[None]), axis=0)) + top
    summed = jnp.sum(every, axis=0)
    lp_p = summed[1:2] - spread[0:1]
    lp_r = summed[3:4] - spread[2:3]
    ratio = lp_p - lp_r
    kl = 0.5 * ratio * ratio
    kl_sum = jnp.sum(jnp.where(inside, kl, 0.0), axis=1, keepdims=True)
    reward = score_col - kl_weight * kl_sum / jnp.maximum(counts, 1.0)
    baseline = jnp.sum(counts * reward, axis=0, keepdims=True) / jnp.sum(
        counts, axis=0, keepdims=True
    )
    advantage = reward - baseline
    lane_doc = iota((docs, LANES), 1).astype(F32)
    out_adv[...] = jnp.sum(
        jnp.where(mine & (rank == lane_doc), advantage, 0.0), axis=0, keepdims=True
    )
    out_lp[...] = col_to_row(jnp.sum(jnp.where(lands, lp_p, 0.0), axis=1, keepdims=True))
    for copy in sends:
        copy.wait_send()


def per_device(
    rows,
    vocab,
    hidden_policy,
    hidden_reference,
    gain_policy,
    gain_reference,
    head_policy,
    head_reference,
    targets,
    loss_mask,
    doc_lengths,
    doc_owner,
    doc_score,
):
    row = lambda a: a.reshape(1, a.shape[0])
    feat = hidden_policy.shape[1]
    width, vcols = head_policy.shape
    z, x = rows // 2, vocab // 2
    n_tok = rows * RESP_DEV
    devices = rows * vocab
    vmem = pl.BlockSpec(memory_space=pltpu.VMEM)
    hbm = pl.BlockSpec(memory_space=pl.ANY)
    dma = pltpu.SemaphoreType.DMA
    lp, adv = pl.pallas_call(
        functools.partial(kernel, rows, vocab),
        out_shape=(
            jax.ShapeDtypeStruct((1, CAP), F32),
            jax.ShapeDtypeStruct((1, LANES), F32),
        ),
        in_specs=[vmem] * 4 + [hbm] * 2 + [vmem] * 5,
        out_specs=(vmem, vmem),
        scratch_shapes=[
            pltpu.VMEM((2, width, vcols), BF16),
            pltpu.VMEM((2, vocab, 2, z, RESP_DEV, feat), BF16),
            pltpu.VMEM((rows, 2, LANES), jnp.int32),
            pltpu.VMEM((devices, 4, n_tok), F32),
            dma((2,)),
            dma((2, 2, x, z)),
            dma((2, 2, x, z)),
            dma((2, 2, x, z)),
            dma((2, 2, x, z)),
            dma((3 * (z + 1),)),
            dma((2, z)),
            dma((2, z)),
            dma((devices,)),
            dma((devices,)),
        ],
        compiler_params=pltpu.CompilerParams(
            collective_id=0, has_side_effects=True, vmem_limit_bytes=60 * 1024 * 1024
        ),
    )(
        hidden_policy,
        hidden_reference,
        gain_policy,
        gain_reference,
        head_policy,
        head_reference,
        row(targets),
        row(loss_mask),
        row(doc_lengths),
        row(doc_owner),
        row(doc_score),
    )
    return lp.reshape(CAP), adv[0, :DOC_DEV]


def solution(mesh):
    return jax.shard_map(
        functools.partial(per_device, mesh.shape["rows"], mesh.shape["vocab"]),
        mesh=mesh,
        in_specs=(
            P("rows", "vocab"),
            P("rows", "vocab"),
            P(),
            P(),
            P(None, ("rows", "vocab")),
            P(None, ("rows", "vocab")),
            P("rows"),
            P("rows"),
            P(),
            P(),
            P(),
        ),
        out_specs=(P("rows"), P("rows")),
        check_vma=False,
    )
```

```python
import functools

import jax
import jax.numpy as jnp
from jax import lax
from jax.experimental import pallas as pl
from jax.experimental.pallas import tpu as pltpu
from jax.sharding import PartitionSpec as P

DOC_DEV = 2
CAP = 128
RESP_DEV = 32

epsilon = 1e-06
kl_weight = 0.1
MESH = pl.DeviceIdType.MESH
F32 = jnp.float32
BF16 = jnp.bfloat16
LANES = 128


def iota(shape, dim):
    return lax.broadcasted_iota(jnp.int32, shape, dim)


def row_to_col(row):
    n = row.shape[1]
    return jnp.sum(jnp.where(iota((n, n), 0) == iota((n, n), 1), row, 0.0), axis=1, keepdims=True)


def col_to_row(col):
    n = col.shape[0]
    return jnp.sum(jnp.where(iota((n, n), 0) == iota((n, n), 1), col, 0.0), axis=0, keepdims=True)


def kernel(
    rows,
    vocab,
    hidden_p,
    hidden_r,
    gain_p,
    gain_r,
    head_p,
    head_r,
    targets,
    mask,
    lengths,
    owners,
    scores,
    out_lp,
    out_adv,
    heads,
    gathered,
    meta,
    stats,
    head_sem,
    send_sem,
    recv_sem,
    core_send,
    core_recv,
    line_send,
    meta_send,
    meta_recv,
    stat_send,
    stat_recv,
):
    Y, C = 2, 2
    Z, X = rows // Y, vocab // C
    tok, feat = hidden_p.shape
    resp = gathered.shape[4]
    n_tok = rows * resp
    vcols = heads.shape[2]
    r, v = lax.axis_index("rows"), lax.axis_index("vocab")
    z, y = r // Y, r % Y
    x, c = v // C, v % C
    devices = rows * vocab
    me = r * vocab + v

    head_copies = [
        pltpu.make_async_copy(src, heads.at[i], head_sem.at[i])
        for i, src in enumerate((head_p, head_r))
    ]
    for copy in head_copies:
        copy.start()

    barrier = pltpu.get_barrier_semaphore()

    def greet(dev):
        pl.semaphore_signal(barrier, inc=1, device_id=dev, device_id_type=MESH)

    greet((r, x * C + 1 - c))
    greet((z * Y + 1 - y, v))
    for dx in range(1, X):
        greet((r, ((x + dx) % X) * C + c))
    for step in range(1, Z):
        greet((((z + step) % Z) * Y + y, v))

    tri = (iota((tok, tok), 0) <= iota((tok, tok), 1)).astype(F32)

    def pick_of(mask_row):
        running = jnp.dot(
            jnp.broadcast_to(mask_row, (8, tok)).astype(BF16),
            tri.astype(BF16),
            preferred_element_type=F32,
        )[0:1]
        slots = iota((resp, tok), 0).astype(F32)
        return ((running - 1.0) == slots) & (mask_row == 1.0)

    own_mask = mask[...].astype(F32)
    own_pick = pick_of(own_mask).astype(BF16)
    for m, hidden in enumerate((hidden_p, hidden_r)):
        gathered[m, v, y, z] = jnp.dot(
            own_pick, hidden[...], preferred_element_type=F32
        ).astype(BF16)
    own_meta = y * Z + z
    meta[own_meta, 0:1, 0:tok] = targets[...]
    meta[own_meta, 1:2, 0:tok] = mask[...]
    pl.semaphore_wait(barrier, X + Z)

    sends = []

    near = jnp.minimum(z, Z - 1 - z)
    order = [z]
    for t in range(1, Z):
        paired = z - (t + 1) // 2 if t % 2 else z + t // 2
        beyond = jnp.where(z > Z - 1 - z, z - (t - near), z + (t - near))
        order.append(jnp.where(t <= 2 * near, paired, beyond))

    def block(m, ay, ax, zz, core):
        return gathered.at[m, ((x + X - ax) % X) * C + core, (y + Y - ay) % Y, zz]

    def remote(src, dst, s_sem, r_sem, dev):
        return pltpu.make_async_remote_copy(
            src_ref=src, dst_ref=dst, send_sem=s_sem, recv_sem=r_sem, device_id=dev, device_id_type=MESH
        )

    def start(ref, s_sem, r_sem, dev):
        copy = remote(ref, ref, s_sem, r_sem, dev)
        copy.start()
        sends.append(copy)

    def send(m, held, moved, zz, dev):
        start(block(m, *held, zz, c), send_sem.at[(m, *moved, zz)], recv_sem.at[(m, *moved, zz)], dev)

    def landed(ref, s_sem, r_sem):
        remote(ref, ref, s_sem, r_sem, (r, v)).wait_recv()

    def arrived(m, ay, ax, zz):
        landed(block(m, ay, ax, zz, c), send_sem.at[m, ay, ax, zz], recv_sem.at[m, ay, ax, zz])

    def to_core(m, ay, ax, zz):
        start(
            block(m, ay, ax, zz, c),
            core_send.at[m, ay, ax, zz],
            core_recv.at[m, ay, ax, zz],
            (r, x * C + 1 - c),
        )

    def along_y(m, ax, zz):
        send(m, (0, ax), (1, ax), zz, (z * Y + 1 - y, v))

    def along_x(m, ay, zz):
        for dx in range(1, X):
            send(m, (ay, 0), (ay, dx), zz, (r, ((x + dx) % X) * C + c))

    def meta_at(ay, zz):
        return meta.at[((y + Y - ay) % Y) * Z + zz]

    def pass_on(t, zz, part):
        if t:
            return
        ref = meta_at(0, zz) if part == 2 else block(part, 0, 0, zz, c)
        r_sem = meta_recv.at[0, zz] if part == 2 else recv_sem.at[part, 0, 0, zz]
        for step in range(1, Z):
            start(ref, line_send.at[part * Z + step], r_sem, (((z + step) % Z) * Y + y, v))

    def second(zz):
        arrived(0, 1, 0, zz)
        along_x(0, 1, zz)
        to_core(0, 1, 0, zz)
        for dx in range(1, X):
            arrived(1, 0, dx, zz)
            along_y(1, dx, zz)
            to_core(1, 0, dx, zz)

    for t, zz in enumerate(order):
        for m in (0, 1):
            if t:
                arrived(m, 0, 0, zz)
            pass_on(t, zz, m)
            if m == 0:
                along_y(0, 0, zz)
            else:
                along_x(1, 0, zz)
                along_x(0, 0, zz)
                along_y(1, 0, zz)
        if t:
            landed(meta_at(0, zz), meta_send.at[0, zz], meta_recv.at[0, zz])
        pass_on(t, zz, 2)
        start(meta_at(0, zz), meta_send.at[1, zz], meta_recv.at[1, zz], (z * Y + 1 - y, v))
        to_core(0, 0, 0, zz)
        to_core(1, 0, 0, zz)
    for zz in order:
        second(zz)
    for zz in order:
        for dx in range(1, X):
            for ay in range(Y):
                arrived(0, ay, dx, zz)
                to_core(0, ay, dx, zz)
        for dx in range(X):
            arrived(1, 1, dx, zz)
            to_core(1, 1, dx, zz)

    for zz in order:
        landed(meta_at(1, zz), meta_send.at[1, zz], meta_recv.at[1, zz])
    target_cols, pos_cols, flag_cols = [], [], []
    for q in range(rows):
        pack = (q % Z) * Y + q // Z
        row_mask = meta[q, 1:2, 0:tok].astype(F32)
        pick = pick_of(row_mask)
        row_targets = meta[q, 0:1, 0:tok].astype(F32)
        where_at = (iota((1, tok), 1) + pack * tok).astype(F32)
        target_cols.append(jnp.sum(jnp.where(pick, row_targets, 0.0), axis=1, keepdims=True))
        pos_cols.append(jnp.sum(jnp.where(pick, where_at, 0.0), axis=1, keepdims=True))
        flag_cols.append(jnp.sum(jnp.where(pick, 1.0, 0.0), axis=1, keepdims=True))
    target_col = jnp.concatenate(target_cols, axis=0)
    pos_col = jnp.concatenate(pos_cols, axis=0)
    flag_col = jnp.concatenate(flag_cols, axis=0)
    base = (me * vcols).astype(F32)
    hit = iota((n_tok, vcols), 1).astype(F32) == (target_col - base)

    stat_cols = []
    for m, gain in enumerate((gain_p, gain_r)):
        for zz in order:
            for ay in range(Y):
                for ax in range(X):
                    landed(
                        block(m, ay, ax, zz, 1 - c),
                        core_send.at[m, ay, ax, zz],
                        core_recv.at[m, ay, ax, zz],
                    )
        head_copies[m].wait()
        total = jnp.zeros((n_tok, 1), F32)
        for part in range(vocab):
            piece = gathered[m, part].reshape(n_tok, feat).astype(F32)
            total = total + jnp.sum(piece * piece, axis=1, keepdims=True)
        inverse_rms = lax.rsqrt(total / (feat * vocab) + epsilon)
        logits = jnp.zeros((n_tok, vcols), F32)
        for part in range(vocab):
            piece = gathered[m, part].reshape(n_tok, feat).astype(F32)
            weight = gain[pl.ds(part * feat, feat)].astype(F32).reshape(1, feat)
            normed = (piece * inverse_rms * weight).astype(BF16)
            logits = logits + jnp.dot(
                normed, heads[m, part * feat : (part + 1) * feat, :], preferred_element_type=F32
            )
        highest = jnp.max(logits, axis=1, keepdims=True)
        lse = highest + jnp.log(jnp.sum(jnp.exp(logits - highest), axis=1, keepdims=True))
        stat_cols += [lse, jnp.sum(jnp.where(hit, logits, 0.0), axis=1, keepdims=True)]

    lane = iota((n_tok, LANES), 1)
    packed = jnp.zeros((n_tok, LANES), F32)
    for i, col in enumerate(stat_cols + [pos_col, flag_col]):
        packed = jnp.where(lane == i, col, packed)
    turned = jnp.transpose(packed)
    stats[me] = turned[0:4]
    pos, flag = turned[4:5], turned[5:6]

    docs = lengths.shape[1]
    length_row = lengths[...].astype(F32)
    owner_row = owners[...].astype(F32)
    length_col, owner_col = row_to_col(length_row), row_to_col(owner_row)
    score_col = row_to_col(scores[...])
    earlier = iota((docs, docs), 1) < iota((docs, docs), 0)
    starts = jnp.sum(jnp.where(earlier, length_row, 0.0), axis=1, keepdims=True)
    before = earlier & (owner_col == owner_row)
    offset = jnp.sum(jnp.where(before, length_row, 0.0), axis=1, keepdims=True)
    rank = jnp.sum(jnp.where(before, 1.0, 0.0), axis=1, keepdims=True)
    inside = (pos >= starts) & (pos < starts + length_col) & (flag == 1.0)
    counts = jnp.sum(jnp.where(inside, 1.0, 0.0), axis=1, keepdims=True)
    mine = owner_col == r.astype(F32)
    slot = jnp.sum(
        jnp.where(inside & mine, offset + pos - starts + 1.0, 0.0), axis=0, keepdims=True
    )
    lands = iota((CAP, n_tok), 0).astype(F32) == slot - 1.0

    for step in range(1, devices):
        other = (me + step) % devices
        copy = remote(
            stats.at[me],
            stats.at[me],
            stat_send.at[step],
            stat_recv.at[step],
            (other // vocab, other % vocab),
        )
        copy.start()
        sends.append(copy)
    for step in range(1, devices):
        src = (me + devices - step) % devices
        remote(
            stats.at[src], stats.at[src], stat_send.at[step], stat_recv.at[step], (r, v)
        ).wait_recv()

    every = stats[...]
    top = jnp.max(every, axis=0)
    spread = jnp.log(jnp.sum(jnp.exp(every - top[None]), axis=0)) + top
    summed = jnp.sum(every, axis=0)
    lp_p = summed[1:2] - spread[0:1]
    lp_r = summed[3:4] - spread[2:3]
    ratio = lp_p - lp_r
    kl = 0.5 * ratio * ratio
    kl_sum = jnp.sum(jnp.where(inside, kl, 0.0), axis=1, keepdims=True)
    reward = score_col - kl_weight * kl_sum / jnp.maximum(counts, 1.0)
    baseline = jnp.sum(counts * reward, axis=0, keepdims=True) / jnp.sum(
        counts, axis=0, keepdims=True
    )
    advantage = reward - baseline
    lane_doc = iota((docs, LANES), 1).astype(F32)
    out_adv[...] = jnp.sum(
        jnp.where(mine & (rank == lane_doc), advantage, 0.0), axis=0, keepdims=True
    )
    out_lp[...] = col_to_row(jnp.sum(jnp.where(lands, lp_p, 0.0), axis=1, keepdims=True))
    for copy in sends:
        copy.wait_send()


def write_out(lp, adv, out_lp, out_adv):
    out_lp[...] = lp[0]
    out_adv[...] = adv[0, 0:DOC_DEV]


def per_device(
    rows,
    vocab,
    hidden_policy,
    hidden_reference,
    gain_policy,
    gain_reference,
    head_policy,
    head_reference,
    targets,
    loss_mask,
    doc_lengths,
    doc_owner,
    doc_score,
):
    row = lambda a: a.reshape(1, a.shape[0])
    feat = hidden_policy.shape[1]
    width, vcols = head_policy.shape
    z, x = rows // 2, vocab // 2
    n_tok = rows * RESP_DEV
    devices = rows * vocab
    vmem = pl.BlockSpec(memory_space=pltpu.VMEM)
    hbm = pl.BlockSpec(memory_space=pl.ANY)
    dma = pltpu.SemaphoreType.DMA
    lp, adv = pl.pallas_call(
        functools.partial(kernel, rows, vocab),
        out_shape=(
            jax.ShapeDtypeStruct((1, CAP), F32),
            jax.ShapeDtypeStruct((1, LANES), F32),
        ),
        in_specs=[vmem] * 4 + [hbm] * 2 + [vmem] * 5,
        out_specs=(vmem, vmem),
        scratch_shapes=[
            pltpu.VMEM((2, width, vcols), BF16),
            pltpu.VMEM((2, vocab, 2, z, RESP_DEV, feat), BF16),
            pltpu.VMEM((rows, 2, LANES), jnp.int32),
            pltpu.VMEM((devices, 4, n_tok), F32),
            dma((2,)),
            dma((2, 2, x, z)),
            dma((2, 2, x, z)),
            dma((2, 2, x, z)),
            dma((2, 2, x, z)),
            dma((3 * (z + 1),)),
            dma((2, z)),
            dma((2, z)),
            dma((devices,)),
            dma((devices,)),
        ],
        compiler_params=pltpu.CompilerParams(
            collective_id=0, has_side_effects=True, vmem_limit_bytes=60 * 1024 * 1024
        ),
    )(
        hidden_policy,
        hidden_reference,
        gain_policy,
        gain_reference,
        head_policy,
        head_reference,
        row(targets),
        row(loss_mask),
        row(doc_lengths),
        row(doc_owner),
        row(doc_score),
    )
    return pl.pallas_call(
        write_out,
        out_shape=(jax.ShapeDtypeStruct((CAP,), F32), jax.ShapeDtypeStruct((DOC_DEV,), F32)),
        in_specs=[vmem] * 2,
        out_specs=(vmem, vmem),
    )(lp, adv)


def solution(mesh):
    return jax.shard_map(
        functools.partial(per_device, mesh.shape["rows"], mesh.shape["vocab"]),
        mesh=mesh,
        in_specs=(
            P("rows", "vocab"),
            P("rows", "vocab"),
            P(),
            P(),
            P(None, ("rows", "vocab")),
            P(None, ("rows", "vocab")),
            P("rows"),
            P("rows"),
            P(),
            P(),
            P(),
        ),
        out_specs=(P("rows"), P("rows")),
        check_vma=False,
    )
```
